32 devices in a mesh: groups: 2 (over y), date: 4 (over z), rng: 2 (over x), az: 2 (over core).
Axes of the slice: x: 2, y: 2, z: 4, core: 2. Of those that a mesh axis runs over, the one named last changes fastest.
Arguments:
- slc: bfloat16 [2, 8, 64, 5120], P(None, ('groups', 'date'), 'az', 'rng'), parts along dimension 1, may hold values from -24 to 24
- offsets: int32 [8, 2], P(('groups', 'date')), parts along dimension 0, may hold values from -24 to 24, as said below
- kernel_index: int32 [8, 2], P(('groups', 'date')), parts along dimension 0, may hold values from 0 to 15
- range_shift: float32 [8], P('groups'), parts along dimension 0, may hold values from -0.15 to 0.15
Outputs:
- ifg: float32 [2, 8, 8, 16, 256], P(None, ('groups', 'date'), None, 'az', 'rng'), parts along dimension 1
The draws below stay inside these ranges and needn't reach their ends.
There are 2 independent parts, one for each index of `groups`. The reference program is written for one: setup_inputs(seed, part) draws one part's arguments, and reference() takes and returns one part's arrays. A program takes and returns all parts, laid end to end along the dimension named above; each array names one. Nothing has to cross between parts.
Inputs may be any that keep to these rules, and one draw needn't show every extreme that they name: `offsets`: column 0 is the azimuth offset, within -8 to 8; column 1 is the range offset. Both ends of both ranges are taken by some date.
All inputs are finite; a program needn't handle non-finite values.
Results may differ from the reference program's by a relative error of at most 0.0039.
Values may be sent and summed in bfloat16 or wider, within the bound.
A program may use at most 64 MiB of HBM per device.

```python
import jax
import jax.numpy as jnp
from jax import lax

LAGS = 8
MAX_AZ = 8
MAX_RG = 24
KERNELS = 16
FILTER_HALF = 8
LOOK_AZ = 4
LOOK_RG = 20
HALO_AZ = 12
HALO_RG = 36
DATES = 4
AZ = 64
RG = 5120


def draw_offsets(key, part):
    line_key, column_key, ranking_key = jax.random.split(key, 3)
    line_shift = jax.random.randint(line_key, (DATES,), -MAX_AZ, MAX_AZ + 1)
    column_shift = jax.random.randint(column_key, (DATES,), -MAX_RG, MAX_RG + 1)
    ranking = jax.random.permutation(ranking_key, DATES)
    line_shift = line_shift.at[ranking[0]].set(MAX_AZ).at[ranking[1]].set(-MAX_AZ)
    column_shift = column_shift.at[ranking[2]].set(MAX_RG).at[ranking[3]].set(-MAX_RG)
    return jnp.stack([line_shift, column_shift], axis=1).astype(jnp.int32)


def touch_ends(result, stream_key, least, largest):
    index_at = [jax.random.randint(jax.random.fold_in(stream_key, axis), (), 0, length) for axis, length in enumerate(result.shape)]
    longest = result.shape.index(max(result.shape))
    next_to = index_at[:longest] + [(index_at[longest] + 1) % result.shape[longest]] + index_at[longest + 1:]
    return result.at[tuple(index_at)].set(least).at[tuple(next_to)].set(largest)


def steps_of(stream_key, dims, pieces, smallest, high):
    level, own = 1.0, jax.random.fold_in(stream_key, 6)
    for dim, blocks in pieces:
        heights = jnp.exp(jax.random.uniform(jax.random.fold_in(own, dim), (blocks,), jnp.float32, smallest / len(pieces), high / len(pieces)))
        level = level * jnp.repeat(heights, dims[dim] // blocks).reshape([-1 if axis == dim else 1 for axis in range(len(dims))])
    return level


def scatter_about(key, shape, deviation, limit, cuts=(), held_as=jnp.bfloat16):
    loudness = steps_of(key, shape, cuts, -0.22, 0.18) if cuts else 1.0
    drawn = jax.random.normal(key, shape, jnp.float32) * deviation * loudness
    return jnp.minimum(jnp.maximum(drawn, -limit), limit).astype(held_as)


def setup_inputs(seed: int = 0, part: int = 0) -> dict:
    streams_of = jax.random.split(jax.random.key(seed), 5)
    part_keys = jax.random.split(jax.random.fold_in(streams_of[4], part), 5)
    slc = scatter_about(part_keys[0], (2, DATES, AZ, RG), 4.0, 24.0, ((1, 4), (2, 2), (3, 2)))
    offsets = draw_offsets(jax.random.fold_in(jax.random.fold_in(streams_of[4], part), 71), part)
    kernel_index = touch_ends(jax.random.randint(part_keys[2], (DATES, 2), 0, KERNELS), jax.random.fold_in(part_keys[2], 1), 0, KERNELS - 1).astype(jnp.int32)
    range_shift = jnp.clip(jax.random.uniform(part_keys[3], (DATES,), jnp.float32, -0.15, 0.15), -0.15, 0.15)
    return {"slc": slc, "offsets": offsets, "kernel_index": kernel_index, "range_shift": range_shift}


def kernel_taps(index):
    fraction = index.astype(jnp.float32) / KERNELS
    position = jnp.arange(8, dtype=jnp.float32) - 3.0 - fraction
    shaped = jnp.sinc(position) * (0.5 + 0.5 * jnp.cos(jnp.pi * position / 5.0))
    return shaped / jnp.sum(shaped)


def lowpass_taps(band_gap):
    spacing = jnp.arange(2 * FILTER_HALF + 1, dtype=jnp.float32) - FILTER_HALF
    window = 0.4 * jnp.sinc(0.4 * spacing) * (0.54 + 0.46 * jnp.cos(jnp.pi * spacing / (FILTER_HALF + 1)))
    phase_angle = jnp.pi * band_gap * spacing
    return window * jnp.cos(phase_angle), window * jnp.sin(phase_angle)


def resample(source, shift_pair, kernel_pair, line_count, column_count):
    span_width = column_count + 2 * FILTER_HALF
    line_start = (HALO_AZ + shift_pair[0] - 3).astype(jnp.int32)
    column_start = (HALO_RG - FILTER_HALF + shift_pair[1] - 3).astype(jnp.int32)
    window = lax.dynamic_slice(source, (jnp.int32(0), line_start, column_start), (2, line_count + 7, span_width + 7)).astype(jnp.float32)
    column_taps = kernel_taps(kernel_pair[1])
    line_taps = kernel_taps(kernel_pair[0])
    across = sum(column_taps[q] * window[:, :, q:q + span_width] for q in range(8))
    return sum(line_taps[p] * across[:, p:p + line_count, :] for p in range(8)).astype(jnp.bfloat16)


def spectral_gap(range_shift, own_date, other_date):
    own_value = lax.dynamic_index_in_dim(range_shift, own_date, 0, keepdims=False)
    other_value = lax.dynamic_index_in_dim(range_shift, other_date, 0, keepdims=False)
    return own_value - other_value


def pair_looks(master, partner, band_gap):
    cos_taps, sin_taps = lowpass_taps(band_gap)
    column_count = master.shape[-1] - 2 * FILTER_HALF
    line_count = master.shape[1]
    master_re = jnp.zeros((line_count, column_count), jnp.float32)
    master_im = master_re
    partner_re = master_re
    partner_im = master_re
    for t in range(2 * FILTER_HALF + 1):
        first_part = master[:, :, t:t + column_count].astype(jnp.float32)
        second_part = partner[:, :, t:t + column_count].astype(jnp.float32)
        master_re = master_re + cos_taps[t] * first_part[0] + sin_taps[t] * first_part[1]
        master_im = master_im + cos_taps[t] * first_part[1] - sin_taps[t] * first_part[0]
        partner_re = partner_re + cos_taps[t] * second_part[0] - sin_taps[t] * second_part[1]
        partner_im = partner_im + cos_taps[t] * second_part[1] + sin_taps[t] * second_part[0]
    product = jnp.stack([master_re * partner_re + master_im * partner_im, master_im * partner_re - master_re * partner_im])
    blocks = product.reshape(2, line_count // LOOK_AZ, LOOK_AZ, column_count // LOOK_RG, LOOK_RG)
    return jnp.mean(blocks, axis=(2, 4))


def reference(slc, offsets, kernel_index, range_shift):
    padded = jnp.pad(slc, ((0, 0), (0, 0), (HALO_AZ, HALO_AZ), (HALO_RG, HALO_RG)))

    def one_resample(inputs):
        source, shift_pair, kernel_pair = inputs
        return resample(source, shift_pair, kernel_pair, AZ, RG)

    resampled = lax.map(one_resample, (jnp.moveaxis(padded, 1, 0), offsets, kernel_index))

    def one_date(date_index):
        master = lax.dynamic_index_in_dim(resampled, date_index, 0, keepdims=False)
        lag_looks = []
        for step_ahead in range(1, LAGS + 1):
            target = date_index + step_ahead
            chosen = jnp.minimum(target, DATES - 1)
            partner = lax.dynamic_index_in_dim(resampled, chosen, 0, keepdims=False)
            usable = (target < DATES).astype(jnp.float32)
            lag_looks.append(pair_looks(master, partner, spectral_gap(range_shift, date_index, chosen)) * usable)
        return jnp.stack(lag_looks, axis=1)

    stacked = lax.map(one_date, jnp.arange(DATES, dtype=jnp.int32))
    return jnp.moveaxis(stacked, 0, 1)
```

```python
import functools

import jax
import jax.numpy as jnp
from jax import lax
from jax.experimental import pallas as pl
from jax.experimental.pallas import tpu as pltpu
from jax.sharding import PartitionSpec as P

LAGS = 8
KERNELS = 16
FILTER_HALF = 8
LOOK_AZ = 4
LOOK_RG = 20
HALO_AZ = 12
HALO_RG = 36


def padded(cells, sides, width):
    for axis, dim in sides:
        count = lax.axis_size(axis)
        ends = count - 1
        head = lax.slice_in_dim(cells, 0, width, axis=dim)
        tail = lax.slice_in_dim(cells, cells.shape[dim] - width, cells.shape[dim], axis=dim)
        cells = jnp.concatenate(
            [
                lax.ppermute(tail, axis, [(i, (i + 1) % count) for i in range(ends)]),
                cells,
                lax.ppermute(head, axis, [((i + 1) % count, i) for i in range(ends)]),
            ],
            axis=dim,
        )
    return cells


def shifted(value, axis, steps):
    count = lax.axis_size(axis)
    leading, last = (max(0, -steps), min(count, count - steps))
    return lax.ppermute(value, axis, [(source, source + steps) for source in range(leading, last)])


def kernel_taps(index):
    fraction = index.astype(jnp.float32) / KERNELS
    position = jnp.arange(8, dtype=jnp.float32) - 3.0 - fraction
    shaped = jnp.sinc(position) * (0.5 + 0.5 * jnp.cos(jnp.pi * position / 5.0))
    return shaped / jnp.sum(shaped)


def lowpass_taps(band_gap):
    spacing = jnp.arange(2 * FILTER_HALF + 1, dtype=jnp.float32) - FILTER_HALF
    window = (
        0.4
        * jnp.sinc(0.4 * spacing)
        * (0.54 + 0.46 * jnp.cos(jnp.pi * spacing / (FILTER_HALF + 1)))
    )
    phase_angle = jnp.pi * band_gap * spacing
    return (window * jnp.cos(phase_angle), window * jnp.sin(phase_angle))


def resample(source, shift_pair, kernel_pair, line_count, column_count):
    span_width = column_count + 2 * FILTER_HALF
    line_start = HALO_AZ + shift_pair[0] - 3
    column_start = HALO_RG - FILTER_HALF + shift_pair[1] - 3
    window = lax.dynamic_slice(
        source, (jnp.int32(0), line_start, column_start), (2, line_count + 7, span_width + 7)
    ).astype(jnp.float32)
    column_taps = kernel_taps(kernel_pair[1])
    line_taps = kernel_taps(kernel_pair[0])
    across = sum((column_taps[q] * window[:, :, q : q + span_width] for q in range(8)))
    return sum((line_taps[p] * across[:, p : p + line_count, :] for p in range(8))).astype(
        jnp.bfloat16
    )


def spectral_gap(range_shift, own_date, other_date):
    own_value = lax.dynamic_index_in_dim(range_shift, own_date, 0, keepdims=False)
    other_value = lax.dynamic_index_in_dim(range_shift, other_date, 0, keepdims=False)
    return own_value - other_value


def pair_looks(master, partner, band_gap):
    cos_taps, sin_taps = lowpass_taps(band_gap)
    column_count = master.shape[-1] - 2 * FILTER_HALF
    line_count = master.shape[1]
    master_re = jnp.zeros((line_count, column_count), jnp.float32)
    master_im = master_re
    partner_re = master_re
    partner_im = master_re
    for t in range(2 * FILTER_HALF + 1):
        first_part = master[:, :, t : t + column_count].astype(jnp.float32)
        second_part = partner[:, :, t : t + column_count].astype(jnp.float32)
        master_re = master_re + cos_taps[t] * first_part[0] + sin_taps[t] * first_part[1]
        master_im = master_im + cos_taps[t] * first_part[1] - sin_taps[t] * first_part[0]
        partner_re = partner_re + cos_taps[t] * second_part[0] - sin_taps[t] * second_part[1]
        partner_im = partner_im + cos_taps[t] * second_part[1] + sin_taps[t] * second_part[0]
    product = jnp.stack(
        [
            master_re * partner_re + master_im * partner_im,
            master_im * partner_re - master_re * partner_im,
        ]
    )
    blocks = product.reshape(2, line_count // LOOK_AZ, LOOK_AZ, column_count // LOOK_RG, LOOK_RG)
    return jnp.mean(blocks, axis=(2, 4))


def shifted_pairs(
    arrived, resampled, range_shift, first_date, date_total, per_device, line_count, padded_width
):
    gathered = jnp.concatenate(arrived, axis=1)

    def one_pair(pair_index):
        within = pair_index // LAGS
        later = within + pair_index % LAGS + 1
        master = lax.dynamic_index_in_dim(resampled, within, 1, keepdims=False)
        partner = lax.dynamic_index_in_dim(gathered, later, 1, keepdims=False).reshape(
            2, line_count, padded_width
        )
        chosen = jnp.minimum(first_date + later, date_total - 1)
        band_gap = spectral_gap(range_shift, first_date + within, chosen)
        return pair_looks(master, partner, band_gap)

    looks = lax.map(one_pair, jnp.arange(per_device * LAGS, dtype=jnp.int32))
    looks = looks.reshape((per_device, LAGS) + looks.shape[1:])
    return jnp.transpose(looks, (2, 0, 1, 3, 4))


TILE = 128
HALF_TILE = TILE // 2
EDGE = 16
MESH = pl.DeviceIdType.MESH


def sinc_of(value):
    angle = jnp.pi * value
    nonzero = jnp.where(angle == 0.0, 1.0, angle)
    return jnp.where(angle == 0.0, 1.0, jnp.sin(nonzero) / nonzero)


def interpolation_shape(position):
    return sinc_of(position) * (0.5 + 0.5 * jnp.cos(jnp.pi * position / 5.0))


def halves(value):
    high = value.astype(jnp.bfloat16)
    low = (value - high.astype(jnp.float32)).astype(jnp.bfloat16)
    return high, low


def toeplitz(reversed_row):
    spread = jnp.broadcast_to(reversed_row, (TILE, TILE))
    rolled = pltpu.roll(spread, 0, 1, stride=1, stride_axis=0)
    row = lax.broadcasted_iota(jnp.int32, (TILE, TILE), 0)
    column = lax.broadcasted_iota(jnp.int32, (TILE, TILE), 1)
    upper = jnp.where(row >= column, rolled, 0.0)
    lower = jnp.where(row < column, rolled, 0.0)
    return jnp.concatenate([upper, lower], axis=0)


def fused_kernel(
    dates,
    lags,
    offset_ref,
    index_ref,
    shift_ref,
    slc_ref,
    out_ref,
    cells,
    across,
    outgoing,
    bursts,
    filters,
    look_matrix,
    products,
    looks_out,
    looks_in,
    local_sem,
    halo_send,
    halo_recv,
    burst_send,
    burst_recv,
    looks_send,
    looks_recv,
):
    lines = slc_ref.shape[1]
    columns = slc_ref.shape[2]
    tiles = columns // TILE
    spans = tiles + 1
    share = lines // dates
    groups = share // LOOK_AZ
    az = lax.axis_index("az")
    rng = lax.axis_index("rng")
    date = lax.axis_index("date")

    barrier = pltpu.get_barrier_semaphore()
    peers = [{"az": 1 - az}, {"rng": 1 - rng}, {"az": 1 - az, "rng": 1 - rng}]
    later = [lax.rem(date + k, dates) for k in range(dates)]
    peers += [{"date": later[k]} for k in range(1, dates)]
    for peer in peers:
        pl.semaphore_signal(barrier, inc=1, device_id=peer, device_id_type=MESH)

    own = pltpu.make_async_copy(
        slc_ref, cells.at[:, pl.ds(EDGE, lines), pl.ds(TILE, columns)], local_sem
    )
    own.start()
    pl.semaphore_wait(barrier, len(peers))

    bottom = EDGE + lines
    right = TILE + columns
    from_line = pl.multiple_of((lines - EDGE) * (1 - az), EDGE)
    to_line = pl.multiple_of(bottom * az, EDGE)
    from_column = pl.multiple_of((columns - TILE) * (1 - rng), TILE)
    to_column = pl.multiple_of(right * rng, TILE)
    halo = []
    for n, (source, target) in enumerate(
        [
            (
                slc_ref.at[:, pl.ds(from_line, EDGE), :],
                cells.at[:, pl.ds(to_line, EDGE), pl.ds(TILE, columns)],
            ),
            (
                slc_ref.at[:, :, pl.ds(from_column, TILE)],
                cells.at[:, pl.ds(EDGE, lines), pl.ds(to_column, TILE)],
            ),
            (
                slc_ref.at[:, pl.ds(from_line, EDGE), pl.ds(from_column, TILE)],
                cells.at[:, pl.ds(to_line, EDGE), pl.ds(to_column, TILE)],
            ),
        ]
    ):
        copy = pltpu.make_async_remote_copy(
            src_ref=source,
            dst_ref=target,
            send_sem=halo_send.at[n],
            recv_sem=halo_recv.at[n],
            device_id=peers[n],
            device_id_type=MESH,
        )
        copy.start()
        halo.append(copy)

    cells[:, pl.ds(to_line, EDGE), :] = jnp.zeros((2, EDGE, cells.shape[2]), jnp.bfloat16)
    cells[:, :, pl.ds(to_column, TILE)] = jnp.zeros((2, cells.shape[1], TILE), jnp.bfloat16)

    lane = lax.broadcasted_iota(jnp.int32, (8, TILE), 1)
    reach = HALF_TILE - lane
    tap = reach - offset_ref[0, 1] + 3
    fraction = index_ref[0, 1].astype(jnp.float32) / KERNELS
    shaped = interpolation_shape(tap.astype(jnp.float32) - 3.0 - fraction)
    shaped = jnp.where((tap >= 0) & (tap < 8), shaped, 0.0)
    column_taps = shaped / jnp.sum(shaped, axis=1, keepdims=True)
    column_high, column_low = halves(toeplitz(column_taps[0:1]))
    column_matrix = jnp.concatenate([column_high, column_low], axis=1)

    position = lax.broadcasted_iota(jnp.int32, (8, TILE), 0).astype(jnp.float32) - 3.0
    shaped = interpolation_shape(position - index_ref[0, 0].astype(jnp.float32) / KERNELS)
    line_taps = shaped / jnp.sum(shaped, axis=0, keepdims=True)

    own.wait()
    for copy in halo:
        copy.wait()

    height = cells.shape[1]
    for j in range(spans):
        window = cells[:, :, j * TILE : (j + 2) * TILE].reshape(2 * height, 2 * TILE)
        both = jnp.dot(window, column_matrix, preferred_element_type=jnp.float32)
        both = both[:, :TILE] + both[:, TILE:]
        across[0, j] = both[:height]
        across[1, j] = both[height:]

    def resampled_share(which):
        start = EDGE - 3 + which * share + offset_ref[0, 0]
        parts = []
        for c in range(2):
            total = None
            for p in range(8):
                term = line_taps[p : p + 1] * across[c, :, pl.ds(start + p, share), :]
                total = term if total is None else total + term
            parts.append(total)
        return jnp.concatenate(parts, axis=1).astype(jnp.bfloat16)

    copies = []
    for k in range(1, dates):
        outgoing[k - 1] = resampled_share(later[k])
        copy = pltpu.make_async_remote_copy(
            src_ref=outgoing.at[k - 1],
            dst_ref=bursts.at[date],
            send_sem=burst_send.at[k - 1],
            recv_sem=burst_recv.at[k - 1],
            device_id={"date": later[k]},
            device_id_type=MESH,
        )
        copy.start()
        copies.append(copy)
    bursts[date] = resampled_share(date)

    pairs = [(d, e) for d in range(dates) for e in range(d + 1, min(dates, d + lags + 1))]
    sublane = lax.broadcasted_iota(jnp.int32, (8, TILE), 0)
    spacing = reach.astype(jnp.float32)
    window = 0.4 * sinc_of(0.4 * spacing)
    window = window * (0.54 + 0.46 * jnp.cos(jnp.pi * spacing / (FILTER_HALF + 1)))
    window = jnp.where(jnp.abs(reach) <= FILTER_HALF, window, 0.0)
    for first in range(0, len(pairs), 8):
        gaps = jnp.zeros((8, TILE), jnp.float32)
        for n, (d, e) in enumerate(pairs[first : first + 8]):
            gaps = jnp.where(sublane == n, shift_ref[d] - shift_ref[e], gaps)
        phase = jnp.pi * gaps * spacing
        even = window * jnp.cos(phase)
        odd = window * jnp.sin(phase)
        for n in range(len(pairs[first : first + 8])):
            even_high, even_low = halves(toeplitz(even[n : n + 1]))
            odd_high, odd_low = halves(toeplitz(odd[n : n + 1]))
            filters[first + n, 0 : 2 * TILE, 0:TILE] = even_high
            filters[first + n, 2 * TILE :, 0:TILE] = even_low
            filters[first + n, 0 : 2 * TILE, TILE:] = odd_high
            filters[first + n, 2 * TILE :, TILE:] = odd_low
    for t in range(tiles):
        column = t * TILE + lax.broadcasted_iota(jnp.int32, (TILE, TILE), 0)
        look = LOOK_RG * lax.broadcasted_iota(jnp.int32, (TILE, TILE), 1)
        inside = (column >= look) & (column < look + LOOK_RG)
        look_matrix[t * TILE : (t + 1) * TILE, :] = jnp.where(inside, 1.0, 0.0).astype(
            jnp.bfloat16
        )

    for copy in copies:
        copy.wait_recv()

    def filtered(which, n):
        held = bursts[which]
        paired = jnp.concatenate([held[:tiles], held[1:]], axis=2)
        paired = paired.reshape(tiles * 2 * share, 2 * TILE)
        total = jnp.dot(paired, filters[n, : 2 * TILE], preferred_element_type=jnp.float32)
        total = total + jnp.dot(
            paired, filters[n, 2 * TILE :], preferred_element_type=jnp.float32
        )
        total = total.reshape(tiles, 2 * share, 2 * TILE)
        return (
            total[:, :share, :TILE],
            total[:, share:, :TILE],
            total[:, :share, TILE:],
            total[:, share:, TILE:],
        )

    rows = 2 * share
    low_start = len(pairs) * rows
    for n, (d, e) in enumerate(pairs):
        even_re, even_im, odd_re, odd_im = filtered(d, n)
        master_re = even_re + odd_im
        master_im = even_im - odd_re
        even_re, even_im, odd_re, odd_im = filtered(e, n)
        partner_re = even_re - odd_im
        partner_im = even_im + odd_re
        product = jnp.concatenate(
            [
                master_re * partner_re + master_im * partner_im,
                master_im * partner_re - master_re * partner_im,
            ],
            axis=1,
        )
        high, low = halves(product)
        products[:, n * rows : (n + 1) * rows, :] = high
        products[:, low_start + n * rows : low_start + (n + 1) * rows, :] = low

    summed = None
    for t in range(0, tiles, 2):
        block = jnp.concatenate([products[t], products[t + 1]], axis=1)
        term = jnp.dot(
            block,
            look_matrix[t * TILE : (t + 2) * TILE, :],
            preferred_element_type=jnp.float32,
        )
        summed = term if summed is None else summed + term
    summed = (summed[:low_start] + summed[low_start:]) / (LOOK_AZ * LOOK_RG)
    total = summed
    for m in range(1, LOOK_AZ):
        total = total + pltpu.roll(summed, low_start - m, 0)

    looks_out[...] = jnp.zeros(looks_out.shape, jnp.float32)
    for n, (d, e) in enumerate(pairs):
        for c in range(2):
            for g in range(groups):
                source = n * rows + c * share + g * LOOK_AZ
                target = ((e - d - 1) * 2 + c) * groups + g
                looks_out[d, target : target + 1, :] = total[source : source + 1]

    returns = []
    for k in range(1, dates):
        copy = pltpu.make_async_remote_copy(
            src_ref=looks_out.at[later[k]],
            dst_ref=looks_in.at[date],
            send_sem=looks_send.at[k - 1],
            recv_sem=looks_recv.at[k - 1],
            device_id={"date": later[k]},
            device_id_type=MESH,
        )
        copy.start()
        returns.append(copy)
    looks_in[date] = looks_out[date]
    out_ref[...] = jnp.zeros(out_ref.shape, jnp.float32)
    for copy in returns:
        copy.wait_recv()
    for i in range(dates):
        for j in range(lags):
            for c in range(2):
                source = (j * 2 + c) * groups
                out_ref[c, j, i * groups : (i + 1) * groups, :] = looks_in[
                    i, source : source + groups, :
                ]
    for copy in copies + returns:
        copy.wait_send()


def fused_fits(slc):
    dates = lax.axis_size("date")
    lines, columns = slc.shape[2], slc.shape[3]
    return (
        lax.axis_size("az") == 2
        and lax.axis_size("rng") == 2
        and slc.shape[1] == 1
        and lines == 8 * dates
        and lines >= 2 * EDGE
        and columns == LOOK_RG * TILE
        and 1 < dates <= LAGS
    )


def fused(slc, offsets, kernel_index, range_shift):
    dates = lax.axis_size("date")
    lags = min(LAGS, dates - 1)
    lines, columns = slc.shape[2], slc.shape[3]
    tiles = columns // TILE
    spans = tiles + 1
    share = lines // dates
    groups = share // LOOK_AZ
    pairs = sum(min(lags, dates - 1 - d) for d in range(dates))
    look_rows = -(-lags * 2 * groups // 8) * 8
    scratch = [
        pltpu.VMEM((2, lines + 2 * EDGE, columns + 2 * TILE), jnp.bfloat16),
        pltpu.VMEM((2, spans, lines + 2 * EDGE, TILE), jnp.float32),
        pltpu.VMEM((dates - 1, spans, 2 * share, TILE), jnp.bfloat16),
        pltpu.VMEM((dates, spans, 2 * share, TILE), jnp.bfloat16),
        pltpu.VMEM((pairs, 4 * TILE, 2 * TILE), jnp.bfloat16),
        pltpu.VMEM((columns, TILE), jnp.bfloat16),
        pltpu.VMEM((tiles, 2 * pairs * 2 * share, TILE), jnp.bfloat16),
        pltpu.VMEM((dates, look_rows, TILE), jnp.float32),
        pltpu.VMEM((dates, look_rows, TILE), jnp.float32),
        pltpu.SemaphoreType.DMA,
        pltpu.SemaphoreType.DMA((3,)),
        pltpu.SemaphoreType.DMA((3,)),
        pltpu.SemaphoreType.DMA((dates - 1,)),
        pltpu.SemaphoreType.DMA((dates - 1,)),
        pltpu.SemaphoreType.DMA((dates - 1,)),
        pltpu.SemaphoreType.DMA((dates - 1,)),
    ]
    smem = pl.BlockSpec(memory_space=pltpu.SMEM)
    looks = pl.pallas_call(
        functools.partial(fused_kernel, dates, lags),
        out_shape=jax.ShapeDtypeStruct((2, LAGS, lines // LOOK_AZ, TILE), jnp.float32),
        in_specs=[smem, smem, smem, pl.BlockSpec(memory_space=pl.ANY)],
        out_specs=pl.BlockSpec(memory_space=pltpu.VMEM),
        scratch_shapes=scratch,
        compiler_params=pltpu.CompilerParams(collective_id=0, has_side_effects=True),
    )(offsets, kernel_index, range_shift, slc.reshape(2, lines, columns))
    return looks.reshape(2, 1, LAGS, lines // LOOK_AZ, TILE)


def body(slc, offsets, kernel_index, range_shift):
    if fused_fits(slc):
        return fused(slc, offsets, kernel_index, range_shift)
    with_lines = padded(slc, (("az", 2),), HALO_AZ)
    widened = padded(with_lines, (("rng", 3),), HALO_RG)
    per_device = slc.shape[1]
    line_count = slc.shape[2]
    column_count = slc.shape[3]
    padded_width = column_count + 2 * FILTER_HALF
    date_devices = lax.axis_size("date")
    first_date = lax.axis_index("date") * per_device
    date_total = date_devices * per_device
    resampled = jnp.stack(
        [resample(widened[:, 0], offsets[0], kernel_index[0], line_count, column_count)], axis=1
    )
    packed = resampled.reshape(2, per_device, line_count * padded_width)
    device_reach = (per_device - 1 + LAGS) // per_device
    arrived = [packed]
    current = packed
    for hop_count in range(device_reach):
        current = shifted(current, "date", -1)
        arrived.append(current)
    return shifted_pairs(
        arrived,
        resampled,
        range_shift,
        first_date,
        date_total,
        per_device,
        line_count,
        padded_width,
    )


def solution(mesh):
    return jax.shard_map(
        body,
        mesh=mesh,
        in_specs=(
            P(None, ("groups", "date"), "az", "rng"),
            P(("groups", "date"), None),
            P(("groups", "date"), None),
            P("groups"),
        ),
        out_specs=P(None, ("groups", "date"), None, "az", "rng"),
        check_vma=False,
    )
```

```python
import functools

import jax
import jax.numpy as jnp
from jax import lax
from jax.experimental import pallas as pl
from jax.experimental.pallas import tpu as pltpu
from jax.sharding import PartitionSpec as P

LAGS = 8
KERNELS = 16
FILTER_HALF = 8
LOOK_AZ = 4
LOOK_RG = 20
HALO_AZ = 12
HALO_RG = 36


def padded(cells, sides, width):
    for axis, dim in sides:
        count = lax.axis_size(axis)
        ends = count - 1
        head = lax.slice_in_dim(cells, 0, width, axis=dim)
        tail = lax.slice_in_dim(cells, cells.shape[dim] - width, cells.shape[dim], axis=dim)
        cells = jnp.concatenate(
            [
                lax.ppermute(tail, axis, [(i, (i + 1) % count) for i in range(ends)]),
                cells,
                lax.ppermute(head, axis, [((i + 1) % count, i) for i in range(ends)]),
            ],
            axis=dim,
        )
    return cells


def shifted(value, axis, steps):
    count = lax.axis_size(axis)
    leading, last = (max(0, -steps), min(count, count - steps))
    return lax.ppermute(value, axis, [(source, source + steps) for source in range(leading, last)])


def kernel_taps(index):
    fraction = index.astype(jnp.float32) / KERNELS
    position = jnp.arange(8, dtype=jnp.float32) - 3.0 - fraction
    shaped = jnp.sinc(position) * (0.5 + 0.5 * jnp.cos(jnp.pi * position / 5.0))
    return shaped / jnp.sum(shaped)


def lowpass_taps(band_gap):
    spacing = jnp.arange(2 * FILTER_HALF + 1, dtype=jnp.float32) - FILTER_HALF
    window = (
        0.4
        * jnp.sinc(0.4 * spacing)
        * (0.54 + 0.46 * jnp.cos(jnp.pi * spacing / (FILTER_HALF + 1)))
    )
    phase_angle = jnp.pi * band_gap * spacing
    return (window * jnp.cos(phase_angle), window * jnp.sin(phase_angle))


def resample(source, shift_pair, kernel_pair, line_count, column_count):
    span_width = column_count + 2 * FILTER_HALF
    line_start = HALO_AZ + shift_pair[0] - 3
    column_start = HALO_RG - FILTER_HALF + shift_pair[1] - 3
    window = lax.dynamic_slice(
        source, (jnp.int32(0), line_start, column_start), (2, line_count + 7, span_width + 7)
    ).astype(jnp.float32)
    column_taps = kernel_taps(kernel_pair[1])
    line_taps = kernel_taps(kernel_pair[0])
    across = sum((column_taps[q] * window[:, :, q : q + span_width] for q in range(8)))
    return sum((line_taps[p] * across[:, p : p + line_count, :] for p in range(8))).astype(
        jnp.bfloat16
    )


def spectral_gap(range_shift, own_date, other_date):
    own_value = lax.dynamic_index_in_dim(range_shift, own_date, 0, keepdims=False)
    other_value = lax.dynamic_index_in_dim(range_shift, other_date, 0, keepdims=False)
    return own_value - other_value


def pair_looks(master, partner, band_gap):
    cos_taps, sin_taps = lowpass_taps(band_gap)
    column_count = master.shape[-1] - 2 * FILTER_HALF
    line_count = master.shape[1]
    master_re = jnp.zeros((line_count, column_count), jnp.float32)
    master_im = master_re
    partner_re = master_re
    partner_im = master_re
    for t in range(2 * FILTER_HALF + 1):
        first_part = master[:, :, t : t + column_count].astype(jnp.float32)
        second_part = partner[:, :, t : t + column_count].astype(jnp.float32)
        master_re = master_re + cos_taps[t] * first_part[0] + sin_taps[t] * first_part[1]
        master_im = master_im + cos_taps[t] * first_part[1] - sin_taps[t] * first_part[0]
        partner_re = partner_re + cos_taps[t] * second_part[0] - sin_taps[t] * second_part[1]
        partner_im = partner_im + cos_taps[t] * second_part[1] + sin_taps[t] * second_part[0]
    product = jnp.stack(
        [
            master_re * partner_re + master_im * partner_im,
            master_im * partner_re - master_re * partner_im,
        ]
    )
    blocks = product.reshape(2, line_count // LOOK_AZ, LOOK_AZ, column_count // LOOK_RG, LOOK_RG)
    return jnp.mean(blocks, axis=(2, 4))


def shifted_pairs(
    arrived, resampled, range_shift, first_date, date_total, per_device, line_count, padded_width
):
    gathered = jnp.concatenate(arrived, axis=1)

    def one_pair(pair_index):
        within = pair_index // LAGS
        later = within + pair_index % LAGS + 1
        master = lax.dynamic_index_in_dim(resampled, within, 1, keepdims=False)
        partner = lax.dynamic_index_in_dim(gathered, later, 1, keepdims=False).reshape(
            2, line_count, padded_width
        )
        chosen = jnp.minimum(first_date + later, date_total - 1)
        band_gap = spectral_gap(range_shift, first_date + within, chosen)
        return pair_looks(master, partner, band_gap)

    looks = lax.map(one_pair, jnp.arange(per_device * LAGS, dtype=jnp.int32))
    looks = looks.reshape((per_device, LAGS) + looks.shape[1:])
    return jnp.transpose(looks, (2, 0, 1, 3, 4))


TILE = 128
HALF_TILE = TILE // 2
EDGE = 16
MESH = pl.DeviceIdType.MESH


def sinc_of(value):
    angle = jnp.pi * value
    nonzero = jnp.where(angle == 0.0, 1.0, angle)
    return jnp.where(angle == 0.0, 1.0, jnp.sin(nonzero) / nonzero)


def interpolation_shape(position):
    return sinc_of(position) * (0.5 + 0.5 * jnp.cos(jnp.pi * position / 5.0))


def halves(value):
    high = value.astype(jnp.bfloat16)
    low = (value - high.astype(jnp.float32)).astype(jnp.bfloat16)
    return high, low


def toeplitz(reversed_row):
    spread = jnp.broadcast_to(reversed_row, (TILE, TILE))
    rolled = pltpu.roll(spread, 0, 1, stride=1, stride_axis=0)
    row = lax.broadcasted_iota(jnp.int32, (TILE, TILE), 0)
    column = lax.broadcasted_iota(jnp.int32, (TILE, TILE), 1)
    upper = jnp.where(row >= column, rolled, 0.0)
    lower = jnp.where(row < column, rolled, 0.0)
    return jnp.concatenate([upper, lower], axis=0)


def flipped(value, mask):
    bit = 1
    result = value
    while bit <= mask:
        if mask & bit:
            result = result + bit * (1 - 2 * lax.rem(value // bit, 2))
        bit *= 2
    return result


def fused_kernel(
    dates,
    lags,
    segments,
    offset_hbm,
    index_hbm,
    shift_hbm,
    slc_ref,
    out_ref,
    offset_ref,
    index_ref,
    shift_ref,
    cells,
    across,
    outgoing,
    bursts,
    filters,
    look_matrix,
    looks_out,
    looks_in,
    small_sem,
    local_sem,
    halo_send,
    halo_recv,
    burst_send,
    burst_recv,
    looks_send,
    looks_recv,
    rising,
    falling,
):
    lines = slc_ref.shape[1]
    columns = slc_ref.shape[2]
    tiles = columns // TILE
    spans = tiles + 1
    share = lines // dates
    groups = share // LOOK_AZ
    az = lax.axis_index("az")
    rng = lax.axis_index("rng")
    date = lax.axis_index("date")

    barrier = pltpu.get_barrier_semaphore()
    peers = [{"az": 1 - az}, {"rng": 1 - rng}, {"az": 1 - az, "rng": 1 - rng}]
    for peer in peers:
        pl.semaphore_signal(barrier, inc=1, device_id=peer, device_id_type=MESH)

    @pl.when(date > 0)
    def _():
        pl.semaphore_signal(barrier, inc=1, device_id={"date": date - 1}, device_id_type=MESH)

    @pl.when(date < dates - 1)
    def _():
        pl.semaphore_signal(barrier, inc=1, device_id={"date": date + 1}, device_id_type=MESH)

    small = [
        pltpu.make_async_copy(source, target, small_sem.at[n])
        for n, (source, target) in enumerate(
            [(offset_hbm, offset_ref), (index_hbm, index_ref), (shift_hbm, shift_ref)]
        )
    ]
    for copy in small:
        copy.start()
    own = pltpu.make_async_copy(
        slc_ref, cells.at[:, pl.ds(EDGE, lines), pl.ds(TILE, columns)], local_sem
    )
    own.start()

    bottom = EDGE + lines
    right = TILE + columns
    from_line = pl.multiple_of((lines - EDGE) * (1 - az), EDGE)
    to_line = pl.multiple_of(bottom * az, EDGE)
    edge_line = pl.multiple_of(bottom * (1 - az), EDGE)
    from_column = pl.multiple_of((columns - TILE) * (1 - rng), TILE)
    to_column = pl.multiple_of(right * rng, TILE)
    cells[:, :, pl.ds(to_column, TILE)] = jnp.zeros((2, cells.shape[1], TILE), jnp.bfloat16)
    across[:, :, pl.ds(to_line, EDGE), :] = jnp.zeros((2, spans, EDGE, TILE), jnp.float32)

    inner = jnp.where((date > 0) & (date < dates - 1), 1, 0)
    pl.semaphore_wait(barrier, len(peers) + 1 + inner)
    halo = []
    for n, (source, target) in enumerate(
        [
            (
                slc_ref.at[:, pl.ds(from_line, EDGE), :],
                cells.at[:, pl.ds(to_line, EDGE), pl.ds(TILE, columns)],
            ),
            (
                slc_ref.at[:, :, pl.ds(from_column, TILE)],
                cells.at[:, pl.ds(EDGE, lines), pl.ds(to_column, TILE)],
            ),
            (
                slc_ref.at[:, pl.ds(from_line, EDGE), pl.ds(from_column, TILE)],
                cells.at[:, pl.ds(to_line, EDGE), pl.ds(to_column, TILE)],
            ),
        ]
    ):
        copy = pltpu.make_async_remote_copy(
            src_ref=source,
            dst_ref=target,
            send_sem=halo_send.at[n],
            recv_sem=halo_recv.at[n],
            device_id=peers[n],
            device_id_type=MESH,
        )
        copy.start()
        halo.append(copy)

    @pl.when(date == 0)
    def _():
        pl.semaphore_signal(rising, inc=1, device_id={"date": date + 1}, device_id_type=MESH)

    @pl.when(date == dates - 1)
    def _():
        pl.semaphore_signal(falling, inc=1, device_id={"date": date - 1}, device_id_type=MESH)

    for copy in small:
        copy.wait()
    lane = lax.broadcasted_iota(jnp.int32, (8, TILE), 1)
    reach = HALF_TILE - lane
    tap = reach - offset_ref[0, 1] + 3
    fraction = index_ref[0, 1].astype(jnp.float32) / KERNELS
    shaped = interpolation_shape(tap.astype(jnp.float32) - 3.0 - fraction)
    shaped = jnp.where((tap >= 0) & (tap < 8), shaped, 0.0)
    column_taps = shaped / jnp.sum(shaped, axis=1, keepdims=True)
    column_high, column_low = halves(toeplitz(column_taps[0:1]))
    column_matrix = jnp.concatenate([column_high, column_low], axis=1)

    position = lax.broadcasted_iota(jnp.int32, (8, TILE), 0).astype(jnp.float32) - 3.0
    shaped = interpolation_shape(position - index_ref[0, 0].astype(jnp.float32) / KERNELS)
    line_taps = shaped / jnp.sum(shaped, axis=0, keepdims=True)

    def range_pass(start, height, which):
        window = jnp.concatenate(
            [
                cells[:, pl.ds(start, height), j * TILE : (j + 2) * TILE].reshape(
                    2 * height, 2 * TILE
                )
                for j in which
            ],
            axis=0,
        )
        both = jnp.dot(window, column_matrix, preferred_element_type=jnp.float32)
        both = (both[:, :TILE] + both[:, TILE:]).reshape(len(which), 2, height, TILE)
        for n, j in enumerate(which):
            for c in range(2):
                across[c, j, pl.ds(start, height), :] = both[n, c]

    own.wait()
    range_pass(EDGE, lines, range(1, spans - 1))

    @pl.when(date > 0)
    def _():
        pl.semaphore_wait(rising, 1)

    @pl.when((date > 0) & (date < dates - 1))
    def _():
        pl.semaphore_signal(rising, inc=1, device_id={"date": date + 1}, device_id_type=MESH)

    @pl.when(date < dates - 1)
    def _():
        pl.semaphore_wait(falling, 1)

    @pl.when((date > 0) & (date < dates - 1))
    def _():
        pl.semaphore_signal(falling, inc=1, device_id={"date": date - 1}, device_id_type=MESH)

    for copy in halo:
        copy.wait_recv()
    range_pass(EDGE, lines, [0, spans - 1])

    def resampled_share(which, low, high):
        start = EDGE - 3 + which * share + offset_ref[0, 0]
        parts = []
        for c in range(2):
            total = None
            for p in range(8):
                term = line_taps[p : p + 1] * across[c, low:high, pl.ds(start + p, share), :]
                total = term if total is None else total + term
            parts.append(total)
        return jnp.concatenate(parts, axis=1).astype(jnp.bfloat16)

    width = tiles // segments
    partners = [flipped(date, mask) for mask in range(dates - 1, 0, -1)]
    sent = []
    for s in range(segments):
        low = 0 if s == 0 else s * width + 1
        high = (s + 1) * width + 1
        range_pass(edge_line, EDGE, range(low, high))
        arriving = []
        for n, partner in enumerate(partners):
            outgoing[n, low:high] = resampled_share(partner, low, high)
            copy = pltpu.make_async_remote_copy(
                src_ref=outgoing.at[n, low:high],
                dst_ref=bursts.at[date, low:high],
                send_sem=burst_send.at[s, n],
                recv_sem=burst_recv.at[s, n],
                device_id={"date": partner},
                device_id_type=MESH,
            )
            copy.start()
            arriving.append(copy)
        bursts[date, low:high] = resampled_share(date, low, high)
        sent.append(arriving)

    pairs = [(d, e) for d in range(dates) for e in range(d + 1, min(dates, d + lags + 1))]
    sublane = lax.broadcasted_iota(jnp.int32, (8, TILE), 0)
    spacing = reach.astype(jnp.float32)
    window = 0.4 * sinc_of(0.4 * spacing)
    window = window * (0.54 + 0.46 * jnp.cos(jnp.pi * spacing / (FILTER_HALF + 1)))
    window = jnp.where(jnp.abs(reach) <= FILTER_HALF, window, 0.0)
    for first in range(0, len(pairs), 8):
        gaps = jnp.zeros((8, TILE), jnp.float32)
        for n, (d, e) in enumerate(pairs[first : first + 8]):
            gaps = jnp.where(sublane == n, shift_ref[d] - shift_ref[e], gaps)
        phase = jnp.pi * gaps * spacing
        even = window * jnp.cos(phase)
        odd = window * jnp.sin(phase)
        for n in range(len(pairs[first : first + 8])):
            even_high, even_low = halves(toeplitz(even[n : n + 1]))
            odd_high, odd_low = halves(toeplitz(odd[n : n + 1]))
            filters[first + n, 0 : 2 * TILE, 0:TILE] = even_high
            filters[first + n, 2 * TILE :, 0:TILE] = even_low
            filters[first + n, 0 : 2 * TILE, TILE:] = odd_high
            filters[first + n, 2 * TILE :, TILE:] = odd_low
    for t in range(tiles):
        column = t * TILE + lax.broadcasted_iota(jnp.int32, (TILE, TILE), 0)
        look = LOOK_RG * lax.broadcasted_iota(jnp.int32, (TILE, TILE), 1)
        inside = (column >= look) & (column < look + LOOK_RG)
        look_matrix[t * TILE : (t + 1) * TILE, :] = jnp.where(inside, 1.0, 0.0).astype(
            jnp.bfloat16
        )
    looks_out[...] = jnp.zeros(looks_out.shape, jnp.float32)
    out_ref[...] = jnp.zeros(out_ref.shape, jnp.float32)

    rows = 2 * share
    summed = None
    for s in range(segments):
        for copy in sent[s]:
            copy.wait_recv()
        low, high = s * width, (s + 1) * width
        windows = []
        for d in range(dates):
            held = bursts[d, low : high + 1]
            paired = jnp.concatenate([held[:width], held[1:]], axis=2)
            windows.append(paired.reshape(width * rows, 2 * TILE))
        highs, lows = [], []
        for n, (d, e) in enumerate(pairs):
            both = jnp.concatenate([windows[d], windows[e]], axis=0)
            total = jnp.dot(both, filters[n, : 2 * TILE], preferred_element_type=jnp.float32)
            total = total + jnp.dot(
                both, filters[n, 2 * TILE :], preferred_element_type=jnp.float32
            )
            total = total.reshape(2, width, rows, 2 * TILE)
            even_re, even_im = total[:, :, :share, :TILE], total[:, :, share:, :TILE]
            odd_re, odd_im = total[:, :, :share, TILE:], total[:, :, share:, TILE:]
            master_re = even_re[0] + odd_im[0]
            master_im = even_im[0] - odd_re[0]
            partner_re = even_re[1] - odd_im[1]
            partner_im = even_im[1] + odd_re[1]
            product = jnp.concatenate(
                [
                    master_re * partner_re + master_im * partner_im,
                    master_im * partner_re - master_re * partner_im,
                ],
                axis=1,
            )
            upper, lower = halves(product)
            highs.append(upper)
            lows.append(lower)
        stacked = jnp.concatenate(highs + lows, axis=1)
        for t in range(0, width, 2):
            step = min(2, width - t)
            block = jnp.concatenate([stacked[t + i] for i in range(step)], axis=1)
            term = jnp.dot(
                block,
                look_matrix[(low + t) * TILE : (low + t + step) * TILE, :],
                preferred_element_type=jnp.float32,
            )
            summed = term if summed is None else summed + term

    middle = len(pairs) * rows
    summed = (summed[:middle] + summed[middle:]) / (LOOK_AZ * LOOK_RG)
    total = summed
    for m in range(1, LOOK_AZ):
        total = total + pltpu.roll(summed, middle - m, 0)
    for n, (d, e) in enumerate(pairs):
        for c in range(2):
            for g in range(groups):
                source = n * rows + c * share + g * LOOK_AZ
                target = ((e - d - 1) * 2 + c) * groups + g
                looks_out[d, target : target + 1, :] = total[source : source + 1]

    returns = []
    for n, partner in enumerate(partners):
        copy = pltpu.make_async_remote_copy(
            src_ref=looks_out.at[partner],
            dst_ref=looks_in.at[date],
            send_sem=looks_send.at[n],
            recv_sem=looks_recv.at[n],
            device_id={"date": partner},
            device_id_type=MESH,
        )
        copy.start()
        returns.append(copy)
    looks_in[date] = looks_out[date]
    for arriving in [halo] + sent:
        for copy in arriving:
            copy.wait_send()
    for copy in returns:
        copy.wait_recv()
    for i in range(dates):
        for j in range(lags):
            for c in range(2):
                source = (j * 2 + c) * groups
                out_ref[c, j, i * groups : (i + 1) * groups, :] = looks_in[
                    i, source : source + groups, :
                ]
    for copy in returns:
        copy.wait_send()


def fused_fits(slc):
    dates = lax.axis_size("date")
    lines, columns = slc.shape[2], slc.shape[3]
    return (
        lax.axis_size("az") == 2
        and lax.axis_size("rng") == 2
        and slc.shape[1] == 1
        and lines == 8 * dates
        and lines >= 2 * EDGE
        and columns == LOOK_RG * TILE
        and dates in (2, 4, 8)
    )


def fused(slc, offsets, kernel_index, range_shift):
    dates = lax.axis_size("date")
    lags = min(LAGS, dates - 1)
    lines, columns = slc.shape[2], slc.shape[3]
    tiles = columns // TILE
    spans = tiles + 1
    share = lines // dates
    groups = share // LOOK_AZ
    pairs = sum(min(lags, dates - 1 - d) for d in range(dates))
    look_rows = -(-lags * 2 * groups // 8) * 8
    segments = 4 if tiles % 4 == 0 else 1
    scratch = [
        pltpu.SMEM(offsets.shape, offsets.dtype),
        pltpu.SMEM(kernel_index.shape, kernel_index.dtype),
        pltpu.SMEM(range_shift.shape, range_shift.dtype),
        pltpu.VMEM((2, lines + 2 * EDGE, columns + 2 * TILE), jnp.bfloat16),
        pltpu.VMEM((2, spans, lines + 2 * EDGE, TILE), jnp.float32),
        pltpu.VMEM((dates - 1, spans, 2 * share, TILE), jnp.bfloat16),
        pltpu.VMEM((dates, spans, 2 * share, TILE), jnp.bfloat16),
        pltpu.VMEM((pairs, 4 * TILE, 2 * TILE), jnp.bfloat16),
        pltpu.VMEM((columns, TILE), jnp.bfloat16),
        pltpu.VMEM((dates, look_rows, TILE), jnp.float32),
        pltpu.VMEM((dates, look_rows, TILE), jnp.float32),
        pltpu.SemaphoreType.DMA((3,)),
        pltpu.SemaphoreType.DMA,
        pltpu.SemaphoreType.DMA((3,)),
        pltpu.SemaphoreType.DMA((3,)),
        pltpu.SemaphoreType.DMA((segments, dates - 1)),
        pltpu.SemaphoreType.DMA((segments, dates - 1)),
        pltpu.SemaphoreType.DMA((dates - 1,)),
        pltpu.SemaphoreType.DMA((dates - 1,)),
        pltpu.SemaphoreType.REGULAR,
        pltpu.SemaphoreType.REGULAR,
    ]
    anywhere = pl.BlockSpec(memory_space=pl.ANY)
    looks = pl.pallas_call(
        functools.partial(fused_kernel, dates, lags, segments),
        out_shape=jax.ShapeDtypeStruct((2, LAGS, lines // LOOK_AZ, TILE), jnp.float32),
        in_specs=[anywhere] * 4,
        out_specs=pl.BlockSpec(memory_space=pltpu.VMEM),
        scratch_shapes=scratch,
        compiler_params=pltpu.CompilerParams(collective_id=0, has_side_effects=True),
    )(offsets, kernel_index, range_shift, slc.reshape(2, lines, columns))
    return looks.reshape(2, 1, LAGS, lines // LOOK_AZ, TILE)


def body(slc, offsets, kernel_index, range_shift):
    if fused_fits(slc):
        return fused(slc, offsets, kernel_index, range_shift)
    with_lines = padded(slc, (("az", 2),), HALO_AZ)
    widened = padded(with_lines, (("rng", 3),), HALO_RG)
    per_device = slc.shape[1]
    line_count = slc.shape[2]
    column_count = slc.shape[3]
    padded_width = column_count + 2 * FILTER_HALF
    date_devices = lax.axis_size("date")
    first_date = lax.axis_index("date") * per_device
    date_total = date_devices * per_device
    resampled = jnp.stack(
        [resample(widened[:, 0], offsets[0], kernel_index[0], line_count, column_count)], axis=1
    )
    packed = resampled.reshape(2, per_device, line_count * padded_width)
    device_reach = (per_device - 1 + LAGS) // per_device
    arrived = [packed]
    current = packed
    for hop_count in range(device_reach):
        current = shifted(current, "date", -1)
        arrived.append(current)
    return shifted_pairs(
        arrived,
        resampled,
        range_shift,
        first_date,
        date_total,
        per_device,
        line_count,
        padded_width,
    )


def solution(mesh):
    return jax.shard_map(
        body,
        mesh=mesh,
        in_specs=(
            P(None, ("groups", "date"), "az", "rng"),
            P(("groups", "date"), None),
            P(("groups", "date"), None),
            P("groups"),
        ),
        out_specs=P(None, ("groups", "date"), None, "az", "rng"),
        check_vma=False,
    )
```

```python
import functools

import jax
import jax.numpy as jnp
from jax import lax
from jax.experimental import pallas as pl
from jax.experimental.pallas import tpu as pltpu
from jax.sharding import PartitionSpec as P

LAGS = 8
KERNELS = 16
FILTER_HALF = 8
LOOK_AZ = 4
LOOK_RG = 20
HALO_AZ = 12
HALO_RG = 36


def padded(cells, sides, width):
    for axis, dim in sides:
        count = lax.axis_size(axis)
        ends = count - 1
        head = lax.slice_in_dim(cells, 0, width, axis=dim)
        tail = lax.slice_in_dim(cells, cells.shape[dim] - width, cells.shape[dim], axis=dim)
        cells = jnp.concatenate(
            [
                lax.ppermute(tail, axis, [(i, (i + 1) % count) for i in range(ends)]),
                cells,
                lax.ppermute(head, axis, [((i + 1) % count, i) for i in range(ends)]),
            ],
            axis=dim,
        )
    return cells


def shifted(value, axis, steps):
    count = lax.axis_size(axis)
    leading, last = (max(0, -steps), min(count, count - steps))
    return lax.ppermute(value, axis, [(source, source + steps) for source in range(leading, last)])


def kernel_taps(index):
    fraction = index.astype(jnp.float32) / KERNELS
    position = jnp.arange(8, dtype=jnp.float32) - 3.0 - fraction
    shaped = jnp.sinc(position) * (0.5 + 0.5 * jnp.cos(jnp.pi * position / 5.0))
    return shaped / jnp.sum(shaped)


def lowpass_taps(band_gap):
    spacing = jnp.arange(2 * FILTER_HALF + 1, dtype=jnp.float32) - FILTER_HALF
    window = (
        0.4
        * jnp.sinc(0.4 * spacing)
        * (0.54 + 0.46 * jnp.cos(jnp.pi * spacing / (FILTER_HALF + 1)))
    )
    phase_angle = jnp.pi * band_gap * spacing
    return (window * jnp.cos(phase_angle), window * jnp.sin(phase_angle))


def resample(source, shift_pair, kernel_pair, line_count, column_count):
    span_width = column_count + 2 * FILTER_HALF
    line_start = HALO_AZ + shift_pair[0] - 3
    column_start = HALO_RG - FILTER_HALF + shift_pair[1] - 3
    window = lax.dynamic_slice(
        source, (jnp.int32(0), line_start, column_start), (2, line_count + 7, span_width + 7)
    ).astype(jnp.float32)
    column_taps = kernel_taps(kernel_pair[1])
    line_taps = kernel_taps(kernel_pair[0])
    across = sum((column_taps[q] * window[:, :, q : q + span_width] for q in range(8)))
    return sum((line_taps[p] * across[:, p : p + line_count, :] for p in range(8))).astype(
        jnp.bfloat16
    )


def spectral_gap(range_shift, own_date, other_date):
    own_value = lax.dynamic_index_in_dim(range_shift, own_date, 0, keepdims=False)
    other_value = lax.dynamic_index_in_dim(range_shift, other_date, 0, keepdims=False)
    return own_value - other_value


def pair_looks(master, partner, band_gap):
    cos_taps, sin_taps = lowpass_taps(band_gap)
    column_count = master.shape[-1] - 2 * FILTER_HALF
    line_count = master.shape[1]
    master_re = jnp.zeros((line_count, column_count), jnp.float32)
    master_im = master_re
    partner_re = master_re
    partner_im = master_re
    for t in range(2 * FILTER_HALF + 1):
        first_part = master[:, :, t : t + column_count].astype(jnp.float32)
        second_part = partner[:, :, t : t + column_count].astype(jnp.float32)
        master_re = master_re + cos_taps[t] * first_part[0] + sin_taps[t] * first_part[1]
        master_im = master_im + cos_taps[t] * first_part[1] - sin_taps[t] * first_part[0]
        partner_re = partner_re + cos_taps[t] * second_part[0] - sin_taps[t] * second_part[1]
        partner_im = partner_im + cos_taps[t] * second_part[1] + sin_taps[t] * second_part[0]
    product = jnp.stack(
        [
            master_re * partner_re + master_im * partner_im,
            master_im * partner_re - master_re * partner_im,
        ]
    )
    blocks = product.reshape(2, line_count // LOOK_AZ, LOOK_AZ, column_count // LOOK_RG, LOOK_RG)
    return jnp.mean(blocks, axis=(2, 4))


def shifted_pairs(
    arrived, resampled, range_shift, first_date, date_total, per_device, line_count, padded_width
):
    gathered = jnp.concatenate(arrived, axis=1)

    def one_pair(pair_index):
        within = pair_index // LAGS
        later = within + pair_index % LAGS + 1
        master = lax.dynamic_index_in_dim(resampled, within, 1, keepdims=False)
        partner = lax.dynamic_index_in_dim(gathered, later, 1, keepdims=False).reshape(
            2, line_count, padded_width
        )
        chosen = jnp.minimum(first_date + later, date_total - 1)
        band_gap = spectral_gap(range_shift, first_date + within, chosen)
        return pair_looks(master, partner, band_gap)

    looks = lax.map(one_pair, jnp.arange(per_device * LAGS, dtype=jnp.int32))
    looks = looks.reshape((per_device, LAGS) + looks.shape[1:])
    return jnp.transpose(looks, (2, 0, 1, 3, 4))


TILE = 128
HALF_TILE = TILE // 2
EDGE = 16
MESH = pl.DeviceIdType.MESH


def sinc_of(value):
    angle = jnp.pi * value
    nonzero = jnp.where(angle == 0.0, 1.0, angle)
    return jnp.where(angle == 0.0, 1.0, jnp.sin(nonzero) / nonzero)


def interpolation_shape(position):
    return sinc_of(position) * (0.5 + 0.5 * jnp.cos(jnp.pi * position / 5.0))


def halves(value):
    high = value.astype(jnp.bfloat16)
    low = (value - high.astype(jnp.float32)).astype(jnp.bfloat16)
    return high, low


def toeplitz(reversed_row):
    spread = jnp.broadcast_to(reversed_row, (TILE, TILE))
    rolled = pltpu.roll(spread, 0, 1, stride=1, stride_axis=0)
    row = lax.broadcasted_iota(jnp.int32, (TILE, TILE), 0)
    column = lax.broadcasted_iota(jnp.int32, (TILE, TILE), 1)
    upper = jnp.where(row >= column, rolled, 0.0)
    lower = jnp.where(row < column, rolled, 0.0)
    return jnp.concatenate([upper, lower], axis=0)


def segment_cuts(tiles):
    if tiles < 8:
        return [tiles]
    return [tiles // 4, tiles * 11 // 20, tiles * 17 // 20, tiles]


def flipped(value, mask):
    bit = 1
    result = value
    while bit <= mask:
        if mask & bit:
            result = result + bit * (1 - 2 * lax.rem(value // bit, 2))
        bit *= 2
    return result


def fused_kernel(
    dates,
    lags,
    offset_hbm,
    index_hbm,
    shift_hbm,
    slc_ref,
    out_ref,
    offset_ref,
    index_ref,
    shift_ref,
    cells,
    across,
    outgoing,
    bursts,
    filters,
    look_matrix,
    looks_out,
    looks_in,
    small_sem,
    local_sem,
    halo_send,
    halo_recv,
    burst_send,
    burst_recv,
    looks_send,
    looks_recv,
    rising,
    falling,
):
    lines = slc_ref.shape[1]
    columns = slc_ref.shape[2]
    tiles = columns // TILE
    spans = tiles + 1
    share = lines // dates
    groups = share // LOOK_AZ
    az = lax.axis_index("az")
    rng = lax.axis_index("rng")
    date = lax.axis_index("date")
    cuts = segment_cuts(tiles)

    barrier = pltpu.get_barrier_semaphore()
    peers = [{"az": 1 - az}, {"rng": 1 - rng}, {"az": 1 - az, "rng": 1 - rng}]
    for peer in peers:
        pl.semaphore_signal(barrier, inc=1, device_id=peer, device_id_type=MESH)

    @pl.when(date > 0)
    def _():
        pl.semaphore_signal(barrier, inc=1, device_id={"date": date - 1}, device_id_type=MESH)

    @pl.when(date < dates - 1)
    def _():
        pl.semaphore_signal(barrier, inc=1, device_id={"date": date + 1}, device_id_type=MESH)

    small = [
        pltpu.make_async_copy(source, target, small_sem.at[n])
        for n, (source, target) in enumerate(
            [(offset_hbm, offset_ref), (index_hbm, index_ref), (shift_hbm, shift_ref)]
        )
    ]
    for copy in small:
        copy.start()
    own = pltpu.make_async_copy(
        slc_ref, cells.at[:, pl.ds(EDGE, lines), pl.ds(TILE, columns)], local_sem
    )
    own.start()

    bottom = EDGE + lines
    right = TILE + columns
    from_line = pl.multiple_of((lines - EDGE) * (1 - az), EDGE)
    to_line = pl.multiple_of(bottom * az, EDGE)
    edge_line = pl.multiple_of(bottom * (1 - az), EDGE)
    from_column = pl.multiple_of((columns - TILE) * (1 - rng), TILE)
    to_column = pl.multiple_of(right * rng, TILE)
    cells[:, :, pl.ds(to_column, TILE)] = jnp.zeros((2, cells.shape[1], TILE), jnp.bfloat16)
    across[:, :, pl.ds(to_line, EDGE), :] = jnp.zeros((2, spans, EDGE, TILE), jnp.float32)

    inner = jnp.where((date > 0) & (date < dates - 1), 1, 0)
    pl.semaphore_wait(barrier, len(peers) + 1 + inner)
    pieces = [
        (
            slc_ref.at[:, :, pl.ds(from_column, TILE)],
            cells.at[:, pl.ds(EDGE, lines), pl.ds(to_column, TILE)],
            peers[1],
        ),
        (
            slc_ref.at[:, pl.ds(from_line, EDGE), pl.ds(from_column, TILE)],
            cells.at[:, pl.ds(to_line, EDGE), pl.ds(to_column, TILE)],
            peers[2],
        ),
    ]
    for s, (first, last) in enumerate(zip([0] + cuts[:-1], cuts)):
        extent = (last - first) * TILE
        piece = (
            slc_ref.at[:, pl.ds(from_line, EDGE), pl.ds(first * TILE, extent)],
            cells.at[:, pl.ds(to_line, EDGE), pl.ds((first + 1) * TILE, extent)],
            peers[0],
        )
        pieces.insert(s if s == 0 else len(pieces), piece)
    halo = []
    for n, (source, target, peer) in enumerate(pieces):
        copy = pltpu.make_async_remote_copy(
            src_ref=source,
            dst_ref=target,
            send_sem=halo_send.at[n],
            recv_sem=halo_recv.at[n],
            device_id=peer,
            device_id_type=MESH,
        )
        copy.start()
        halo.append(copy)

    def relay(step):
        @pl.when((date >= step) & (date < dates - 1))
        def _():
            pl.semaphore_signal(rising, inc=1, device_id={"date": date + 1}, device_id_type=MESH)

        @pl.when((date <= dates - 1 - step) & (date > 0))
        def _():
            pl.semaphore_signal(falling, inc=1, device_id={"date": date - 1}, device_id_type=MESH)

    if dates > 2:
        relay(1)
    for copy in small:
        copy.wait()
    lane = lax.broadcasted_iota(jnp.int32, (8, TILE), 1)
    reach = HALF_TILE - lane
    tap = reach - offset_ref[0, 1] + 3
    fraction = index_ref[0, 1].astype(jnp.float32) / KERNELS
    shaped = interpolation_shape(tap.astype(jnp.float32) - 3.0 - fraction)
    shaped = jnp.where((tap >= 0) & (tap < 8), shaped, 0.0)
    column_taps = shaped / jnp.sum(shaped, axis=1, keepdims=True)
    column_high, column_low = halves(toeplitz(column_taps[0:1]))
    column_matrix = jnp.concatenate([column_high, column_low], axis=1)

    position = lax.broadcasted_iota(jnp.int32, (8, TILE), 0).astype(jnp.float32) - 3.0
    shaped = interpolation_shape(position - index_ref[0, 0].astype(jnp.float32) / KERNELS)
    line_taps = shaped / jnp.sum(shaped, axis=0, keepdims=True)

    def range_pass(start, height, which):
        window = jnp.concatenate(
            [
                cells[:, pl.ds(start, height), j * TILE : (j + 2) * TILE].reshape(
                    2 * height, 2 * TILE
                )
                for j in which
            ],
            axis=0,
        )
        both = jnp.dot(window, column_matrix, preferred_element_type=jnp.float32)
        both = (both[:, :TILE] + both[:, TILE:]).reshape(len(which), 2, height, TILE)
        for n, j in enumerate(which):
            for c in range(2):
                across[c, j, pl.ds(start, height), :] = both[n, c]

    own.wait()
    range_pass(EDGE, lines, range(1, spans - 1))

    for step in range(1, dates - 1):

        @pl.when(date >= step + 1)
        def _():
            pl.semaphore_wait(rising, 1)

        @pl.when(date < dates - 1 - step)
        def _():
            pl.semaphore_wait(falling, 1)

        if step < dates - 2:
            relay(step + 1)

    def resampled_share(which, low, high):
        start = EDGE - 3 + which * share + offset_ref[0, 0]
        parts = []
        for c in range(2):
            total = None
            for p in range(8):
                term = line_taps[p : p + 1] * across[c, low:high, pl.ds(start + p, share), :]
                total = term if total is None else total + term
            parts.append(total)
        return jnp.concatenate(parts, axis=1).astype(jnp.bfloat16)

    masks = [dates // 2] + [m for m in range(dates - 1, 0, -1) if m != dates // 2]
    partners = [flipped(date, mask) for mask in masks]
    bounds = [0] + cuts[:-1] + [spans]
    sent = []
    for s in range(len(cuts)):
        low, high = bounds[s], bounds[s + 1]
        for copy in halo[:3] if s == 0 else halo[s + 2 : s + 3]:
            copy.wait_recv()
        if s == 0:
            range_pass(EDGE, lines, [0])
        if high == spans:
            range_pass(EDGE, lines, [spans - 1])
        range_pass(edge_line, EDGE, range(low, high))
        arriving = []
        for n, partner in enumerate(partners):
            outgoing[n, low:high] = resampled_share(partner, low, high)
            copy = pltpu.make_async_remote_copy(
                src_ref=outgoing.at[n, low:high],
                dst_ref=bursts.at[date, low:high],
                send_sem=burst_send.at[s, n],
                recv_sem=burst_recv.at[s, n],
                device_id={"date": partner},
                device_id_type=MESH,
            )
            copy.start()
            arriving.append(copy)
        bursts[date, low:high] = resampled_share(date, low, high)
        sent.append(arriving)

    pairs = [(d, e) for d in range(dates) for e in range(d + 1, min(dates, d + lags + 1))]
    sublane = lax.broadcasted_iota(jnp.int32, (8, TILE), 0)
    spacing = reach.astype(jnp.float32)
    window = 0.4 * sinc_of(0.4 * spacing)
    window = window * (0.54 + 0.46 * jnp.cos(jnp.pi * spacing / (FILTER_HALF + 1)))
    window = jnp.where(jnp.abs(reach) <= FILTER_HALF, window, 0.0)
    for first in range(0, len(pairs), 8):
        gaps = jnp.zeros((8, TILE), jnp.float32)
        for n, (d, e) in enumerate(pairs[first : first + 8]):
            gaps = jnp.where(sublane == n, shift_ref[d] - shift_ref[e], gaps)
        phase = jnp.pi * gaps * spacing
        even = window * jnp.cos(phase)
        odd = window * jnp.sin(phase)
        for n in range(len(pairs[first : first + 8])):
            even_high, even_low = halves(toeplitz(even[n : n + 1]))
            odd_high, odd_low = halves(toeplitz(odd[n : n + 1]))
            filters[first + n, 0 : 2 * TILE, 0:TILE] = even_high
            filters[first + n, 2 * TILE :, 0:TILE] = even_low
            filters[first + n, 0 : 2 * TILE, TILE:] = odd_high
            filters[first + n, 2 * TILE :, TILE:] = odd_low
    for t in range(tiles):
        column = t * TILE + lax.broadcasted_iota(jnp.int32, (TILE, TILE), 0)
        look = LOOK_RG * lax.broadcasted_iota(jnp.int32, (TILE, TILE), 1)
        inside = (column >= look) & (column < look + LOOK_RG)
        look_matrix[t * TILE : (t + 1) * TILE, :] = jnp.where(inside, 1.0, 0.0).astype(
            jnp.bfloat16
        )
    looks_out[...] = jnp.zeros(looks_out.shape, jnp.float32)
    out_ref[...] = jnp.zeros(out_ref.shape, jnp.float32)

    rows = 2 * share
    summed = None
    for s in range(len(cuts)):
        for copy in sent[s]:
            copy.wait_recv()
        low, high = max(bounds[s] - 1, 0), bounds[s + 1] - 1
        width = high - low
        windows = []
        for d in range(dates):
            held = bursts[d, low : high + 1]
            paired = jnp.concatenate([held[:width], held[1:]], axis=2)
            windows.append(paired.reshape(width * rows, 2 * TILE))
        highs, lows = [], []
        for n, (d, e) in enumerate(pairs):
            both = jnp.concatenate([windows[d], windows[e]], axis=0)
            total = jnp.dot(both, filters[n, : 2 * TILE], preferred_element_type=jnp.float32)
            total = total + jnp.dot(
                both, filters[n, 2 * TILE :], preferred_element_type=jnp.float32
            )
            total = total.reshape(2, width, rows, 2 * TILE)
            even_re, even_im = total[:, :, :share, :TILE], total[:, :, share:, :TILE]
            odd_re, odd_im = total[:, :, :share, TILE:], total[:, :, share:, TILE:]
            master_re = even_re[0] + odd_im[0]
            master_im = even_im[0] - odd_re[0]
            partner_re = even_re[1] - odd_im[1]
            partner_im = even_im[1] + odd_re[1]
            product = jnp.concatenate(
                [
                    master_re * partner_re + master_im * partner_im,
                    master_im * partner_re - master_re * partner_im,
                ],
                axis=1,
            )
            upper, lower = halves(product)
            highs.append(upper)
            lows.append(lower)
        stacked = jnp.concatenate(highs + lows, axis=1)
        for t in range(0, width, 2):
            step = min(2, width - t)
            block = jnp.concatenate([stacked[t + i] for i in range(step)], axis=1)
            term = jnp.dot(
                block,
                look_matrix[(low + t) * TILE : (low + t + step) * TILE, :],
                preferred_element_type=jnp.float32,
            )
            summed = term if summed is None else summed + term

    middle = len(pairs) * rows
    summed = (summed[:middle] + summed[middle:]) / (LOOK_AZ * LOOK_RG)
    total = summed
    for m in range(1, LOOK_AZ):
        total = total + pltpu.roll(summed, middle - m, 0)
    for n, (d, e) in enumerate(pairs):
        for c in range(2):
            for g in range(groups):
                source = n * rows + c * share + g * LOOK_AZ
                target = ((e - d - 1) * 2 + c) * groups + g
                looks_out[d, target : target + 1, :] = total[source : source + 1]

    returns = []
    for n, partner in enumerate(partners):
        copy = pltpu.make_async_remote_copy(
            src_ref=looks_out.at[partner],
            dst_ref=looks_in.at[date],
            send_sem=looks_send.at[n],
            recv_sem=looks_recv.at[n],
            device_id={"date": partner},
            device_id_type=MESH,
        )
        copy.start()
        returns.append(copy)
    looks_in[date] = looks_out[date]
    for arriving in [halo] + sent:
        for copy in arriving:
            copy.wait_send()
    for copy in returns:
        copy.wait_recv()
    for i in range(dates):
        for j in range(lags):
            for c in range(2):
                source = (j * 2 + c) * groups
                out_ref[c, j, i * groups : (i + 1) * groups, :] = looks_in[
                    i, source : source + groups, :
                ]
    for copy in returns:
        copy.wait_send()


def fused_fits(slc):
    dates = lax.axis_size("date")
    lines, columns = slc.shape[2], slc.shape[3]
    return (
        lax.axis_size("az") == 2
        and lax.axis_size("rng") == 2
        and slc.shape[1] == 1
        and lines == 8 * dates
        and lines >= 2 * EDGE
        and columns == LOOK_RG * TILE
        and dates in (2, 4, 8)
    )


def fused(slc, offsets, kernel_index, range_shift):
    dates = lax.axis_size("date")
    lags = min(LAGS, dates - 1)
    lines, columns = slc.shape[2], slc.shape[3]
    tiles = columns // TILE
    spans = tiles + 1
    share = lines // dates
    groups = share // LOOK_AZ
    pairs = sum(min(lags, dates - 1 - d) for d in range(dates))
    look_rows = -(-lags * 2 * groups // 8) * 8
    segments = len(segment_cuts(tiles))
    scratch = [
        pltpu.SMEM(offsets.shape, offsets.dtype),
        pltpu.SMEM(kernel_index.shape, kernel_index.dtype),
        pltpu.SMEM(range_shift.shape, range_shift.dtype),
        pltpu.VMEM((2, lines + 2 * EDGE, columns + 2 * TILE), jnp.bfloat16),
        pltpu.VMEM((2, spans, lines + 2 * EDGE, TILE), jnp.float32),
        pltpu.VMEM((dates - 1, spans, 2 * share, TILE), jnp.bfloat16),
        pltpu.VMEM((dates, spans, 2 * share, TILE), jnp.bfloat16),
        pltpu.VMEM((pairs, 4 * TILE, 2 * TILE), jnp.bfloat16),
        pltpu.VMEM((columns, TILE), jnp.bfloat16),
        pltpu.VMEM((dates, look_rows, TILE), jnp.float32),
        pltpu.VMEM((dates, look_rows, TILE), jnp.float32),
        pltpu.SemaphoreType.DMA((3,)),
        pltpu.SemaphoreType.DMA,
        pltpu.SemaphoreType.DMA((segments + 2,)),
        pltpu.SemaphoreType.DMA((segments + 2,)),
        pltpu.SemaphoreType.DMA((segments, dates - 1)),
        pltpu.SemaphoreType.DMA((segments, dates - 1)),
        pltpu.SemaphoreType.DMA((dates - 1,)),
        pltpu.SemaphoreType.DMA((dates - 1,)),
        pltpu.SemaphoreType.REGULAR,
        pltpu.SemaphoreType.REGULAR,
    ]
    anywhere = pl.BlockSpec(memory_space=pl.ANY)
    looks = pl.pallas_call(
        functools.partial(fused_kernel, dates, lags),
        out_shape=jax.ShapeDtypeStruct((2, LAGS, lines // LOOK_AZ, TILE), jnp.float32),
        in_specs=[anywhere] * 4,
        out_specs=pl.BlockSpec(memory_space=pltpu.VMEM),
        scratch_shapes=scratch,
        compiler_params=pltpu.CompilerParams(collective_id=0, has_side_effects=True),
    )(offsets, kernel_index, range_shift, slc.reshape(2, lines, columns))
    return looks.reshape(2, 1, LAGS, lines // LOOK_AZ, TILE)


def body(slc, offsets, kernel_index, range_shift):
    if fused_fits(slc):
        return fused(slc, offsets, kernel_index, range_shift)
    with_lines = padded(slc, (("az", 2),), HALO_AZ)
    widened = padded(with_lines, (("rng", 3),), HALO_RG)
    per_device = slc.shape[1]
    line_count = slc.shape[2]
    column_count = slc.shape[3]
    padded_width = column_count + 2 * FILTER_HALF
    date_devices = lax.axis_size("date")
    first_date = lax.axis_index("date") * per_device
    date_total = date_devices * per_device
    resampled = jnp.stack(
        [resample(widened[:, 0], offsets[0], kernel_index[0], line_count, column_count)], axis=1
    )
    packed = resampled.reshape(2, per_device, line_count * padded_width)
    device_reach = (per_device - 1 + LAGS) // per_device
    arrived = [packed]
    current = packed
    for hop_count in range(device_reach):
        current = shifted(current, "date", -1)
        arrived.append(current)
    return shifted_pairs(
        arrived,
        resampled,
        range_shift,
        first_date,
        date_total,
        per_device,
        line_count,
        padded_width,
    )


def solution(mesh):
    return jax.shard_map(
        body,
        mesh=mesh,
        in_specs=(
            P(None, ("groups", "date"), "az", "rng"),
            P(("groups", "date"), None),
            P(("groups", "date"), None),
            P("groups"),
        ),
        out_specs=P(None, ("groups", "date"), None, "az", "rng"),
        check_vma=False,
    )
```
